1024 devices in a mesh: dp: 32 (over x, z_hi, core), fsdp: 32 (over y, z_lo).
Axes of the slice: x: 4, y: 4, z: 32 (z_hi: 4, z_lo: 8; z = z_hi * 8 + z_lo), core: 2. Of those that a mesh axis runs over, the one named last changes fastest.
Arguments:
- query_in: bfloat16 [229376, 1024], P(('dp', 'fsdp')), may hold values from -32 to 32
- key_in: bfloat16 [229376, 1024], P(('dp', 'fsdp')), may hold values from -32 to 32
- value_in: bfloat16 [229376, 1024], P(('dp', 'fsdp')), may hold values from -6 to 6
- length_plan: int32 [1024, 224], P(('dp', 'fsdp')), may hold values from 0 to 223, each once within a row
- segment_ids: int32 [1024, 224], P(('dp', 'fsdp')), may hold values from 0 to 3, never falling along the last dimension, each value on 1 to 112 neighbouring positions
- out_grad: bfloat16 [229376, 1024], P(('dp', 'fsdp')), may hold values from -6 to 6
- query_gain: float32 [128], replicated, may hold values from 0.7 to 6
- key_gain: float32 [128], replicated, may hold values from 0.7 to 6
Outputs:
- query_grad: bfloat16 [229376, 1024], P(('dp', 'fsdp'))
- key_grad: bfloat16 [229376, 1024], P(('dp', 'fsdp'))
- value_grad: bfloat16 [229376, 1024], P(('dp', 'fsdp'))
- query_gain_grad: float32 [128], replicated
- key_gain_grad: float32 [128], replicated
The draws below stay inside these ranges and needn't reach their ends.
Inputs may be any that keep to these rules, and one draw needn't show every extreme that they name: `length_plan`: each row is a permutation of 0 to 223. `segment_ids`: within a row the numbers never fall; each utterance piece holds 1 to 112 frames, and one holds exactly 112.
All inputs are finite; a program needn't handle non-finite values.
Results may differ from the reference program's by a relative error of at most 0.01.
The reference program's roundings to bfloat16 on the way count: a program that leaves them out, or rounds other values in their place, can miss the bound.
Values may be sent and summed in bfloat16 or wider, within the bound.
No kernel may reach another device: no remote copies, remote signals or barrier semaphores. Data moves between devices by JAX's collectives and lax.ppermute only.
A program may use at most 32 MiB of HBM per device.

```python
import math
import jax
import jax.numpy as jnp
import numpy as np
from jax import lax

HEADS = 8
HEAD = 128
TOK_DEV = 224
SEGMENTS = 4
HID = 1024
SEGMAX = 112
DEVROWS = 1024
FRAMES = 229376
N_DP = 32
N_FSDP = 32


def query_key_fields(key):
    base_key = jax.random.fold_in(key, 101)
    subkeys = jax.random.split(base_key, 5)
    width = HEADS * HEAD
    col_scale = jnp.exp(jax.random.uniform(subkeys[0], (HEAD,), jnp.float32, jnp.log(0.4), jnp.log(4.0)))
    col_scale = jnp.tile(col_scale, HEADS)
    row_query = jnp.exp(jax.random.uniform(subkeys[1], (FRAMES, 1), jnp.float32, jnp.log(0.3), jnp.log(3.0)))
    row_key = jnp.exp(jax.random.uniform(subkeys[2], (FRAMES, 1), jnp.float32, jnp.log(0.3), jnp.log(3.0)))
    noise_query = jax.random.normal(subkeys[3], (FRAMES, width), jnp.float32)
    noise_key = jax.random.normal(subkeys[4], (FRAMES, width), jnp.float32)
    key_field = noise_key
    query_field = noise_query
    query_out = jnp.clip(query_field * col_scale * row_query, -32.0, 32.0)
    key_out = jnp.clip(key_field * col_scale * row_key, -32.0, 32.0)
    return (query_out, key_out)


def draw_query_in(key, part):
    return query_key_fields(key)[0].astype(jnp.bfloat16)


def draw_key_in(key, part):
    return query_key_fields(key)[1].astype(jnp.bfloat16)


def draw_gain(key, salt):
    gain_key = jax.random.fold_in(key, salt)
    return jax.random.uniform(gain_key, (HEAD,), jnp.float32, 0.7, 1.6)


def draw_query_gain(key, part):
    return draw_gain(key, 202)


def draw_key_gain(key, part):
    return draw_gain(key, 303)


def block_scale(stream_key, shape, shards, least, largest):
    loudness = 1.0
    for axis_at, parts in shards:
        heights = jax.random.uniform(jax.random.fold_in(jax.random.fold_in(stream_key, 6), axis_at), (parts,), jnp.float32, least / len(shards), largest / len(shards))
        loudness = loudness * jnp.repeat(jnp.exp(heights), shape[axis_at] // parts).reshape((-1,) + (1,) * (len(shape) - 1 - axis_at))
    return loudness


def split_up(amount, total, bound, skew):
    weights = [(1 << 20) // math.isqrt(rank ** skew) + 1 for rank in range(2, amount + 1)]
    surplus, holding = total - bound - (amount - 1), [1] * (amount - 1)
    while surplus > 0:
        free = [i for i in range(amount - 1) if holding[i] < bound]
        mass, remaining = sum([weights[i] for i in free]), surplus
        for i in free:
            more = min(bound - holding[i], max(1, remaining * weights[i] // mass), surplus)
            holding[i] = holding[i] + more
            surplus = surplus - more
    return np.array([bound] + holding)


def ragged_sizes(stream_key, amount, total, limit, slope):
    if amount == 2:
        one = jax.random.randint(stream_key, (), max(1, total - limit), min(limit, total - 1) + 1)
        return jnp.stack([one, total - one])
    tallies = jnp.asarray(split_up(amount, total, limit, slope), jnp.int32)
    pairs = (amount - 1) // 2
    giver, sink = tallies[1:1 + 2 * pairs:2], tallies[2:2 + 2 * pairs:2]
    room = jnp.minimum(giver - 1, limit - sink)
    shifted = jax.random.randint(jax.random.fold_in(stream_key, 1), (pairs,), 0, 1 << 20) % (room + 1)
    tallies = tallies.at[1:1 + 2 * pairs:2].set(giver - shifted).at[2:2 + 2 * pairs:2].set(sink + shifted)
    return tallies[jax.random.permutation(jax.random.fold_in(stream_key, 2), amount)]


def bell_draw(stream_key, shape, scale, limit, shards=(), kind=jnp.bfloat16):
    values = scale * jax.random.normal(stream_key, shape, jnp.float32)
    if shards:
        values = values * block_scale(stream_key, shape, shards, -0.22, 0.18)
    return jnp.clip(values, -limit, limit).astype(kind)


def setup_inputs(seed: int = 0) -> dict:
    seeds = jax.random.split(jax.random.key(seed), 9)
    return {
        "query_in": draw_query_in(jax.random.fold_in(seeds[8], 71), 0),
        "key_in": draw_key_in(jax.random.fold_in(seeds[8], 71), 0),
        "value_in": bell_draw(seeds[2], (FRAMES, HID), 1.0, 6.0, ((0, 1024),)),
        "length_plan": jax.vmap(lambda own: jax.random.permutation(own, TOK_DEV))(jax.random.split(seeds[3], DEVROWS)).reshape((DEVROWS, TOK_DEV)).astype(jnp.int32),
        "segment_ids": jax.vmap(lambda own: jnp.searchsorted(jnp.cumsum(ragged_sizes(own, SEGMENTS, TOK_DEV, SEGMAX, 2)), jnp.arange(TOK_DEV), side="right"))(jax.random.split(seeds[4], DEVROWS)).reshape((DEVROWS, TOK_DEV)).astype(jnp.int32),
        "out_grad": bell_draw(seeds[5], (FRAMES, HID), 1.0, 6.0, ((0, 1024),)),
        "query_gain": draw_query_gain(jax.random.fold_in(seeds[8], 71), 0),
        "key_gain": draw_key_gain(jax.random.fold_in(seeds[8], 71), 0),
    }


def normalize(raw, gain):
    frames = raw.shape[0]
    values = raw.astype(jnp.float32).reshape(frames, HEADS, HEAD)
    inv_rms = lax.rsqrt(lax.optimization_barrier(jnp.mean(values * values, axis=-1, keepdims=True)) + 1e-06)
    unit_vec = values * inv_rms
    rounded = lax.optimization_barrier((unit_vec * gain).astype(jnp.bfloat16))
    return (unit_vec, inv_rms, rounded.astype(jnp.float32))

def norm_back(d_norm, unit_vec, inv_rms, gain):
    d_unit = d_norm * gain
    inner = lax.optimization_barrier(jnp.mean(d_unit * unit_vec, axis=-1, keepdims=True))
    result = inv_rms * (d_unit - unit_vec * inner)
    return result.reshape(result.shape[0], -1).astype(jnp.bfloat16)

def attend(query_in, key_in, value_in, segment_row, out_grad, query_gain, key_gain):
    frames = query_in.shape[0]
    score_scale = HEAD ** (-0.5)
    q_unit, q_inv, q_wide = normalize(query_in, query_gain)
    k_unit, k_inv, k_wide = normalize(key_in, key_gain)
    values_in = value_in.reshape(frames, HEADS, HEAD).astype(jnp.float32)
    grad_heads = out_grad.reshape(frames, HEADS, HEAD).astype(jnp.float32)
    scores = jnp.einsum('thd,shd->hts', q_wide, k_wide) * score_scale
    same_seg = segment_row[:, None] == segment_row[None, :]
    scores = jnp.where(same_seg[None], scores, -jnp.inf)
    row_max = lax.optimization_barrier(jnp.max(scores, axis=-1, keepdims=True))
    exponent = jnp.exp(scores - row_max)
    attn_probs = exponent / lax.optimization_barrier(jnp.sum(exponent, axis=-1, keepdims=True))
    probs_wide = lax.optimization_barrier(attn_probs.astype(jnp.bfloat16)).astype(jnp.float32)
    output = jnp.einsum('hts,shd->thd', probs_wide, values_in)
    row_delta = lax.optimization_barrier(jnp.sum(grad_heads * output, axis=-1))
    value_grad = jnp.einsum('hts,thd->shd', probs_wide, grad_heads).astype(jnp.bfloat16).reshape(frames, -1)
    d_prob = jnp.einsum('thd,shd->hts', grad_heads, values_in)
    d_score = (attn_probs * (d_prob - row_delta.T[:, :, None]) * score_scale).astype(jnp.bfloat16)
    d_score = lax.optimization_barrier(d_score).astype(jnp.float32)
    d_qnorm = jnp.einsum('hts,shd->thd', d_score, k_wide)
    d_knorm = jnp.einsum('hts,thd->shd', d_score, q_wide)
    query_part = lax.optimization_barrier(jnp.sum(d_qnorm * q_unit, axis=(0, 1)))
    key_part = lax.optimization_barrier(jnp.sum(d_knorm * k_unit, axis=(0, 1)))
    query_grad = norm_back(d_qnorm, q_unit, q_inv, query_gain)
    key_grad = norm_back(d_knorm, k_unit, k_inv, key_gain)
    return (query_grad, key_grad, value_grad, query_part, key_part)

def reference(query_in, key_in, value_in, length_plan, segment_ids, out_grad, query_gain, key_gain):
    devices = N_DP * N_FSDP
    block_rows = TOK_DEV // N_DP
    width = query_in.shape[1]
    positions = jnp.arange(TOK_DEV, dtype=jnp.int32)
    inverse = jax.vmap(lambda plan_row: jnp.zeros((TOK_DEV,), jnp.int32).at[plan_row].set(positions))(length_plan)

    def repack(source):
        rows_in = source.reshape(devices, TOK_DEV, width)
        outgoing = jax.vmap(lambda table, index: table[index])(rows_in, inverse)
        outgoing = outgoing.reshape(N_DP, N_FSDP, N_DP, block_rows, width)
        return jnp.transpose(outgoing, (2, 1, 0, 3, 4)).reshape(devices, TOK_DEV, width)
    packed_query = repack(query_in)
    packed_key = repack(key_in)
    packed_value = repack(value_in)
    grad_rows = out_grad.reshape(devices, TOK_DEV, width)

    def attend_device(device_items):
        query_dev, key_dev, value_dev, segment_row, grad_dev = device_items
        return attend(query_dev, key_dev, value_dev, segment_row, grad_dev, query_gain, key_gain)
    query_grad, key_grad, value_grad, query_part, key_part = lax.map(attend_device, (packed_query, packed_key, packed_value, segment_ids, grad_rows))
    return (query_grad.reshape(FRAMES, width), key_grad.reshape(FRAMES, width), value_grad.reshape(FRAMES, width), lax.optimization_barrier(jnp.sum(query_part, axis=0)), lax.optimization_barrier(jnp.sum(key_part, axis=0)))
```

```python
import jax
import jax.numpy as jnp
from jax import lax
from jax.sharding import PartitionSpec as P

HEAD = 128


def normalize(raw, gain):
    frames = raw.shape[0]
    values = raw.astype(jnp.float32).reshape(frames, -1, HEAD)
    inv_rms = lax.rsqrt(jnp.mean(values * values, axis=-1, keepdims=True) + 1e-06)
    unit_vec = values * inv_rms
    return (unit_vec, inv_rms, (unit_vec * gain).astype(jnp.bfloat16))


def norm_back(d_norm, unit_vec, inv_rms, gain):
    d_unit = d_norm * gain
    inner = jnp.mean(d_unit * unit_vec, axis=-1, keepdims=True)
    result = inv_rms * (d_unit - unit_vec * inner)
    return result.reshape(result.shape[0], -1).astype(jnp.bfloat16)


def attend_heads(query_pk, key_pk, value_pk, grad_rows, segment_row, query_gain, key_gain):
    frames = query_pk.shape[0]
    score_scale = HEAD ** (-0.5)
    q_unit, q_inv, q_norm = normalize(query_pk, query_gain)
    k_unit, k_inv, k_norm = normalize(key_pk, key_gain)
    scores = (
        jnp.einsum("thd,shd->hts", q_norm, k_norm, preferred_element_type=jnp.float32) * score_scale
    )
    same_seg = segment_row[:, None] == segment_row[None, :]
    scores = jnp.where(same_seg[None], scores, -jnp.inf)
    row_max = jnp.max(scores, axis=-1, keepdims=True)
    exponent = jnp.exp(scores - row_max)
    attn_probs = exponent / jnp.sum(exponent, axis=-1, keepdims=True)
    value_heads = value_pk.reshape(frames, -1, HEAD)
    grad_heads = grad_rows.reshape(frames, -1, HEAD)
    probs_half = attn_probs.astype(jnp.bfloat16)
    output = jnp.einsum("hts,shd->thd", probs_half, value_heads, preferred_element_type=jnp.float32)
    row_delta = jnp.sum(grad_heads.astype(jnp.float32) * output, axis=-1)
    value_grad = jnp.einsum(
        "hts,thd->shd", probs_half, grad_heads, preferred_element_type=jnp.float32
    )
    value_grad = value_grad.astype(jnp.bfloat16).reshape(frames, -1)
    d_prob = jnp.einsum("thd,shd->hts", grad_heads, value_heads, preferred_element_type=jnp.float32)
    d_score = (attn_probs * (d_prob - row_delta.T[:, :, None]) * score_scale).astype(jnp.bfloat16)
    d_qnorm = jnp.einsum("hts,shd->thd", d_score, k_norm, preferred_element_type=jnp.float32)
    d_knorm = jnp.einsum("hts,thd->shd", d_score, q_norm, preferred_element_type=jnp.float32)
    query_part = jnp.sum(d_qnorm * q_unit, axis=(0, 1))
    key_part = jnp.sum(d_knorm * k_unit, axis=(0, 1))
    query_grad = norm_back(d_qnorm, q_unit, q_inv, query_gain)
    key_grad = norm_back(d_knorm, k_unit, k_inv, key_gain)
    return (query_grad, key_grad, value_grad, query_part, key_part)


def plane_and_line_groups():
    def flat(x, z_hi, core, y, z_lo):
        return ((x * 4 + z_hi) * 2 + core) * 32 + y * 8 + z_lo

    plane = [
        [flat(x, z_hi, core, y, z_lo) for x in range(4) for y in range(4) for core in range(2)]
        for z_hi in range(4)
        for z_lo in range(8)
    ]
    line = [
        [flat(x, z_hi, core, y, z_lo) for z_hi in range(4) for z_lo in range(8)]
        for x in range(4)
        for y in range(4)
        for core in range(2)
    ]
    return plane, line


def sum_over_all(part):
    for groups in plane_and_line_groups():
        spread = jnp.broadcast_to(part, (len(groups[0]), *part.shape))
        spread = lax.all_to_all(
            spread, ("dp", "fsdp"), 0, 0, axis_index_groups=groups, tiled=True
        )
        part = jnp.sum(lax.optimization_barrier(spread), axis=0)
    return part


def on_device(query_in, key_in, value_in, length_plan, segment_ids, out_grad, query_gain, key_gain):
    frames, width = query_in.shape
    groups = lax.axis_size("dp")
    positions = jnp.arange(frames, dtype=jnp.int32)
    inverse = jnp.zeros((frames,), jnp.int32).at[length_plan[0]].set(positions)
    sends = [source[inverse].reshape(groups, -1, HEAD) for source in (query_in, key_in, value_in)]
    got = lax.all_to_all(jnp.concatenate(sends, axis=1), "dp", 0, 0, tiled=True)
    query_pk, key_pk, value_pk = (part.reshape(frames, width) for part in jnp.split(got, 3, axis=1))
    query_grad, key_grad, value_grad, query_part, key_part = attend_heads(
        query_pk, key_pk, value_pk, out_grad, segment_ids[0], query_gain, key_gain
    )
    query_total, key_total = sum_over_all(jnp.stack([query_part, key_part]))
    return (query_grad, key_grad, value_grad, query_total, key_total)


def solution(mesh):
    in_specs = (
        P(("dp", "fsdp"), None),
        P(("dp", "fsdp"), None),
        P(("dp", "fsdp"), None),
        P(("dp", "fsdp"), None),
        P(("dp", "fsdp"), None),
        P(("dp", "fsdp"), None),
        P(),
        P(),
    )
    out_specs = (
        P(("dp", "fsdp"), None),
        P(("dp", "fsdp"), None),
        P(("dp", "fsdp"), None),
        P(),
        P(),
    )
    return jax.shard_map(
        on_device, mesh=mesh, in_specs=in_specs, out_specs=out_specs, check_vma=False
    )
```

```python
import jax
import jax.numpy as jnp
from jax import lax
from jax.experimental import pallas as pl
from jax.experimental.pallas import tpu as pltpu
from jax.sharding import PartitionSpec as P

HEADS = 8
HEAD = 128
SOURCES = 32
ROWS = 7
SLOTS = 8
TILES = 21
PADDED = SOURCES * SLOTS


def dot(a, b, contract):
    return lax.dot_general(
        a, b, ((contract[:1], contract[1:]), ((), ())), preferred_element_type=jnp.float32
    )


def one_hot(hit):
    return jnp.where(hit, 1.0, 0.0).astype(jnp.bfloat16)


def pack_kernel(plan_ref, query_ref, key_ref, value_ref, out_ref):
    frames = plan_ref.shape[1]
    row = lax.broadcasted_iota(jnp.int32, (PADDED, frames), 0)
    group, slot = row >> 3, row & 7
    plan = jnp.broadcast_to(plan_ref[...], (PADDED, frames))
    pick = one_hot((plan == group * ROWS + slot) & (slot != ROWS))
    spill = value_ref[:, 5 * HEAD :]
    refs = (query_ref, key_ref, value_ref)
    for r in range(ROWS):
        extra = dot(one_hot((plan == group * ROWS + r) & (slot == ROWS)), spill, (1, 0))
        for a in range(3):
            tile = ROWS * a + r
            tensor, head = divmod(tile, HEADS)
            own = dot(pick, refs[tensor][:, head * HEAD : (head + 1) * HEAD], (1, 0))
            both = own + extra[:, a * HEAD : (a + 1) * HEAD]
            out_ref[:, tile] = both.reshape(SOURCES, SLOTS, HEAD).astype(jnp.bfloat16)


def attend_kernel(
    got_ref, segment_ref, grad_ref, query_gain_ref, key_gain_ref,
    query_out, key_out, value_out, part_out,
):
    frames = segment_ref.shape[1]
    scale = HEAD ** (-0.5)
    row = lax.broadcasted_iota(jnp.int32, (PADDED, frames), 0)
    column = lax.broadcasted_iota(jnp.int32, (PADDED, frames), 1)
    hit = (column == row - (row >> 3)) & ((row & 7) != ROWS)
    spread = one_hot(hit)
    segment = jnp.broadcast_to(segment_ref[...], (PADDED, frames)).astype(jnp.float32)
    segment_column = jnp.sum(jnp.where(hit, segment, 0.0), axis=1, keepdims=True)
    pad_column = lax.broadcasted_iota(jnp.int32, (PADDED, 1), 0) & 7
    segment_column = jnp.where(pad_column == ROWS, 9.0, segment_column)
    segment_line = dot(segment[:SLOTS].astype(jnp.bfloat16), spread, (1, 1))[:1]
    pad_line = lax.broadcasted_iota(jnp.int32, (1, PADDED), 1) & 7
    segment_line = jnp.where(pad_line == ROWS, 9.0, segment_line)
    bias = jnp.where(segment_column == segment_line, 0.0, -jnp.inf)

    lane_row = lax.broadcasted_iota(jnp.int32, (SOURCES, SLOTS, HEAD), 1)
    live = lane_row != ROWS

    def tile(index):
        return got_ref[:, index].astype(jnp.float32)

    def own(index):
        return jnp.where(live, tile(index), 0.0).reshape(PADDED, HEAD)

    def spilled(a):
        total = jnp.zeros((SOURCES, SLOTS, HEAD), jnp.float32)
        for r in range(ROWS):
            total = jnp.where(lane_row == r, tile(ROWS * a + r)[:, ROWS:], total)
        return total.reshape(PADDED, HEAD)

    def normalize(raw, gain):
        inverse = lax.rsqrt(jnp.sum(raw * raw, axis=1, keepdims=True) * (1.0 / HEAD) + 1e-06)
        unit = raw * inverse
        return unit, inverse, (unit * gain).astype(jnp.bfloat16)

    def norm_back(d_norm, unit, inverse, gain):
        d_unit = d_norm * gain
        inner = jnp.sum(d_unit * unit, axis=1, keepdims=True) * (1.0 / HEAD)
        return (inverse * (d_unit - unit * inner)).astype(jnp.bfloat16)

    def gather(padded):
        return dot(spread, padded, (0, 0)).astype(jnp.bfloat16)

    query_gain, key_gain = query_gain_ref[...], key_gain_ref[...]
    query_part = jnp.zeros((1, HEAD), jnp.float32)
    key_part = jnp.zeros((1, HEAD), jnp.float32)
    for head in range(HEADS):
        lanes = slice(head * HEAD, (head + 1) * HEAD)
        q_unit, q_inv, q_norm = normalize(own(head), query_gain)
        k_unit, k_inv, k_norm = normalize(own(HEADS + head), key_gain)
        value = own(2 * HEADS + head) if head < 5 else spilled(head - 5)
        value = value.astype(jnp.bfloat16)
        grad_wide = dot(spread, grad_ref[:, lanes], (1, 0))
        grad = grad_wide.astype(jnp.bfloat16)
        scores = dot(q_norm, k_norm, (1, 1)) * scale + bias
        exponent = jnp.exp(scores - jnp.max(scores, axis=1, keepdims=True))
        probs = exponent / jnp.sum(exponent, axis=1, keepdims=True)
        probs_half = probs.astype(jnp.bfloat16)
        output = dot(probs_half, value, (1, 0))
        row_delta = jnp.sum(grad_wide * output, axis=1, keepdims=True)
        value_out[:, lanes] = gather(dot(probs_half, grad, (0, 0)).astype(jnp.bfloat16))
        d_prob = dot(grad, value, (1, 1))
        d_score = (probs * (d_prob - row_delta) * scale).astype(jnp.bfloat16)
        d_qnorm = dot(d_score, k_norm, (1, 0))
        d_knorm = dot(d_score, q_norm, (0, 0))
        query_part += jnp.sum(d_qnorm * q_unit, axis=0, keepdims=True)
        key_part += jnp.sum(d_knorm * k_unit, axis=0, keepdims=True)
        query_out[:, lanes] = gather(norm_back(d_qnorm, q_unit, q_inv, query_gain))
        key_out[:, lanes] = gather(norm_back(d_knorm, k_unit, k_inv, key_gain))
    part_out[:, 0:1, :] = jnp.broadcast_to(query_part[None], (SOURCES, 1, HEAD))
    part_out[:, 1:2, :] = jnp.broadcast_to(key_part[None], (SOURCES, 1, HEAD))


def plane_and_line_groups():
    def flat(x, z_hi, core, y, z_lo):
        return ((x * 4 + z_hi) * 2 + core) * 32 + y * 8 + z_lo

    plane = [
        [flat(x, z_hi, core, y, z_lo) for x in range(4) for y in range(4) for core in range(2)]
        for z_hi in range(4)
        for z_lo in range(8)
    ]
    line = [
        [flat(x, z_hi, core, y, z_lo) for z_hi in range(4) for z_lo in range(8)]
        for x in range(4)
        for y in range(4)
        for core in range(2)
    ]
    return plane, line


def sum_over_all(spread):
    for step, groups in enumerate(plane_and_line_groups()):
        if step:
            spread = jnp.broadcast_to(part, spread.shape)
        spread = lax.all_to_all(
            spread, ("dp", "fsdp"), 0, 0, axis_index_groups=groups, tiled=True
        )
        part = jnp.sum(lax.optimization_barrier(spread), axis=0)
    return part


def on_device(query_in, key_in, value_in, length_plan, segment_ids, out_grad, query_gain, key_gain):
    send = pl.pallas_call(
        pack_kernel,
        out_shape=jax.ShapeDtypeStruct((SOURCES, TILES, SLOTS, HEAD), jnp.bfloat16),
        cost_estimate=pl.CostEstimate(flops=10**9, bytes_accessed=3 * 10**6, transcendentals=0),
        name="pack",
    )(length_plan, query_in, key_in, value_in)
    got = lax.all_to_all(send, "dp", 0, 0, tiled=True)
    like = jax.ShapeDtypeStruct(query_in.shape, jnp.bfloat16)
    query_grad, key_grad, value_grad, parts = pl.pallas_call(
        attend_kernel,
        out_shape=(like, like, like, jax.ShapeDtypeStruct((SOURCES, 2, HEAD), jnp.float32)),
        cost_estimate=pl.CostEstimate(flops=10**9, bytes_accessed=4 * 10**6, transcendentals=10**6),
        name="attend",
    )(got, segment_ids, out_grad, query_gain.reshape(1, HEAD), key_gain.reshape(1, HEAD))
    query_total, key_total = sum_over_all(parts)
    return (query_grad, key_grad, value_grad, query_total, key_total)


def solution(mesh):
    rows = P(("dp", "fsdp"), None)
    return jax.shard_map(
        on_device,
        mesh=mesh,
        in_specs=(rows, rows, rows, rows, rows, rows, P(), P()),
        out_specs=(rows, rows, rows, P(), P()),
        check_vma=False,
    )
```

```python
import jax
import jax.numpy as jnp
from jax import lax
from jax.experimental import pallas as pl
from jax.experimental.pallas import tpu as pltpu
from jax.sharding import PartitionSpec as P


HEADS = 8
HEAD = 128
TURNS = 4
PEERS = 8
ROWS = 7
SLOTS = 8
PADDED = TURNS * PEERS * SLOTS
BF16 = jnp.bfloat16

OWN = (
    [(tensor, head) for head in range(5) for tensor in range(3)] + [(0, 5)],
    [(0, 6), (1, 6), (2, 6), (0, 7), (1, 7)],
)
SPILL = (
    [(1, 5, r) for r in range(7)] + [(2, 5, r) for r in range(7)] + [(2, 7, 5), (2, 7, 6)],
    [(2, 7, r) for r in range(5)],
)
CUT = 6 * HEAD


def dot(a, b, contract):
    return lax.dot_general(
        a, b, ((contract[:1], contract[1:]), ((), ())), preferred_element_type=jnp.float32
    )


def one_hot(hit):
    return jnp.where(hit, 1.0, 0.0).astype(BF16)


def place():
    return (lax.axis_index("dp") >> 1) & 3


def pack_kernel(part, plan_ref, query_ref, key_ref, value_ref, *out_refs):
    frames = plan_ref.shape[1]
    row = lax.broadcasted_iota(jnp.int32, (PADDED, frames), 0)
    dest = ((row >> 4) & 3) * 8 + ((place() + (row >> 6)) & 3) * 2 + ((row >> 3) & 1)
    slot = row & 7
    plan = jnp.broadcast_to(plan_ref[...], (PADDED, frames))
    pick = one_hot((plan == dest * ROWS + slot) & (slot != ROWS))
    refs = (query_ref, key_ref, value_ref)
    first = 0 if part == 0 else 6

    def lanes(tensor, head):
        at = (head - first) * HEAD
        return refs[tensor][:, at : at + HEAD]

    by_frame = {}
    for tile, spill in enumerate(SPILL[part]):
        by_frame.setdefault(spill[2], []).append((tile, *spill[:2]))
    for frame, tiles in by_frame.items():
        late = one_hot((plan == dest * ROWS + frame) & (slot == ROWS))
        for tile, tensor, head in tiles:
            both = dot(pick, lanes(*OWN[part][tile]), (1, 0))
            both += dot(late, lanes(tensor, head), (1, 0))
            both = both.reshape(TURNS, PEERS, SLOTS, HEAD).astype(BF16)
            for turn in range(TURNS):
                out_refs[turn][:, tile] = both[turn]


def attend_kernel(part, got_ref, *refs):
    if part == 0:
        segment_ref, grad_ref, query_gain_ref, key_gain_ref = refs[:4]
        outs, (query_pad, key_pad, value_pad, grad_pad) = refs[4:8], refs[8:]
    else:
        rest_ref, before_ref, segment_ref, grad_ref, query_gain_ref, key_gain_ref = refs[:6]
        outs, (query_pad, key_pad, value_pad, grad_pad) = refs[9:13], refs[13:]
    query_out, key_out, value_out, part_out = outs
    frames = segment_ref.shape[1]
    scale = HEAD ** (-0.5)
    exp2_scale = scale * 1.4426950408889634
    here = place()

    def frame_of(row):
        source = (row >> 6) * 8 + ((here - (row >> 3)) & 3) * 2 + ((row >> 5) & 1)
        return jnp.where((row & 7) == ROWS, -1, source * ROWS + (row & 7))

    row = lax.broadcasted_iota(jnp.int32, (PADDED, 1), 0)
    line = lax.broadcasted_iota(jnp.int32, (1, PADDED), 1)
    hit = lax.broadcasted_iota(jnp.int32, (PADDED, frames), 1) == frame_of(row)
    spread = one_hot(hit)
    gather = one_hot(lax.broadcasted_iota(jnp.int32, (frames, PADDED), 0) == frame_of(line))
    segment = jnp.broadcast_to(segment_ref[...], (PADDED, frames)).astype(jnp.float32)
    segment_row = jnp.sum(jnp.where(hit, segment, 0.0), axis=1, keepdims=True)
    segment_row = jnp.where((row & 7) == ROWS, 9.0, segment_row)
    segment_line = dot(segment[:SLOTS].astype(BF16), spread, (1, 1))[:1]
    segment_line = jnp.where((line & 7) == ROWS, 9.0, segment_line)
    bias = jnp.where(segment_row == segment_line, 0.0, -jnp.inf)
    grad_pad[...] = dot(spread, grad_ref[...], (1, 0)).astype(BF16)
    slot = lax.broadcasted_iota(jnp.int32, (PEERS, TURNS, SLOTS, HEAD), 2)

    def fetch(tensor, head):
        if (tensor, head) in OWN[part]:
            return got_ref[:, :, OWN[part].index((tensor, head))].reshape(PADDED, HEAD)
        total = None
        for r in range(ROWS):
            if (tensor, head, r) in SPILL[part]:
                tile = got_ref[:, :, SPILL[part].index((tensor, head, r))]
            else:
                tile = rest_ref[:, :, SPILL[0].index((tensor, head, r)) - 14]
            spilled = jnp.broadcast_to(tile.astype(jnp.float32)[:, :, ROWS:], slot.shape)
            total = spilled if total is None else jnp.where(slot == r, spilled, total)
        return total.reshape(PADDED, HEAD).astype(BF16)

    def normalize(raw, gain):
        raw = raw.astype(jnp.float32)
        inverse = lax.rsqrt(jnp.sum(raw * raw, axis=1, keepdims=True) * (1.0 / HEAD) + 1e-06)
        unit = raw * inverse
        return unit, inverse, (unit * gain).astype(BF16)

    def norm_back(d_norm, unit, inverse, gain):
        d_unit = d_norm * gain
        inner = jnp.sum(d_unit * unit, axis=1, keepdims=True) * (1.0 / HEAD)
        return (inverse * (d_unit - unit * inner)).astype(BF16)

    query_gain, key_gain = query_gain_ref[...], key_gain_ref[...]
    query_part = jnp.zeros((1, HEAD), jnp.float32)
    key_part = jnp.zeros((1, HEAD), jnp.float32)
    first, last = (0, 6) if part == 0 else (6, HEADS)
    for head in range(first, last):
        lanes = slice((head - first) * HEAD, (head - first + 1) * HEAD)
        q_unit, q_inv, q_norm = normalize(fetch(0, head), query_gain)
        k_unit, k_inv, k_norm = normalize(fetch(1, head), key_gain)
        value = fetch(2, head)
        grad = grad_pad[:, lanes]
        halves, scores_grad = [], []
        for start in range(0, PADDED, HEAD):
            block = slice(start, start + HEAD)
            scores = dot(k_norm, q_norm[block], (1, 1)) + bias[:, block]
            scores = (scores - jnp.max(scores, axis=0, keepdims=True)) * exp2_scale
            exponent = jnp.exp2(scores)
            probs = exponent * (1.0 / jnp.sum(exponent, axis=0, keepdims=True))
            half = probs.astype(BF16)
            d_prob = dot(value, grad[block], (1, 1))
            row_delta = jnp.sum(half.astype(jnp.float32) * d_prob, axis=0, keepdims=True)
            d_score = (probs * (d_prob - row_delta) * scale).astype(BF16)
            halves.append(half)
            scores_grad.append(d_score)
        probs_half = jnp.concatenate(halves, axis=1)
        d_score = jnp.concatenate(scores_grad, axis=1)
        value_pad[:, lanes] = dot(probs_half, grad, (1, 0)).astype(BF16)
        d_qnorm = dot(d_score, k_norm, (0, 0))
        d_knorm = dot(d_score, q_norm, (1, 0))
        query_part += jnp.sum(d_qnorm * q_unit, axis=0, keepdims=True)
        key_part += jnp.sum(d_knorm * k_unit, axis=0, keepdims=True)
        query_pad[:, lanes] = norm_back(d_qnorm, q_unit, q_inv, query_gain)
        key_pad[:, lanes] = norm_back(d_knorm, k_unit, k_inv, key_gain)
    parts = jnp.concatenate([query_part, key_part], axis=0)
    if part == 0:
        part_out[...] = parts
    else:
        part_out[...] = jnp.broadcast_to((before_ref[...] + parts)[None], part_out.shape)
    for padded, out in ((query_pad, query_out), (key_pad, key_out), (value_pad, value_out)):
        out[...] = dot(gather, padded[...], (1, 0)).astype(BF16)


def whole(shape):
    return pl.BlockSpec(shape, lambda i: (0,) * len(shape))


def lane_block(part):
    return pl.BlockSpec((224, CUT), lambda i: (0, 0)) if part == 0 else pl.BlockSpec(
        (224, HEADS * HEAD - CUT), lambda i: (0, 3)
    )


def pack_call(part, plan, query_in, key_in, value_in):
    tiles = len(OWN[part])
    shape = (PEERS, tiles, SLOTS, HEAD)
    value_block = whole(value_in.shape) if part == 0 else lane_block(1)
    return pl.pallas_call(
        lambda *refs: pack_kernel(part, *refs),
        grid=(1,),
        in_specs=[whole(plan.shape), lane_block(part), lane_block(part), value_block],
        out_specs=[whole(shape)] * TURNS,
        out_shape=[jax.ShapeDtypeStruct(shape, BF16)] * TURNS,
        cost_estimate=pl.CostEstimate(
            flops=5 * 10**7 * tiles, bytes_accessed=13 * 10**4 * tiles, transcendentals=0
        ),
    )(plan, query_in, key_in, value_in)


def attend_call(part, got, before, segment_ids, out_grad, query_gain, key_gain):
    like = jax.ShapeDtypeStruct(out_grad.shape, BF16)
    heads = 6 if part == 0 else 2
    padded = pltpu.VMEM((PADDED, heads * HEAD), BF16)
    args = [got]
    specs = [whole(got.shape)]
    part_shape = (2, HEAD) if part == 0 else (TURNS * PEERS, 2, HEAD)
    aliases = {}
    if part == 1:
        got_before, *grads, parts = before
        args += [got_before, parts]
        specs += [
            pl.BlockSpec((PEERS, TURNS, 2, SLOTS, HEAD), lambda i: (0, 0, 7, 0, 0)),
            whole(parts.shape),
        ]
    args += [segment_ids, out_grad, query_gain.reshape(1, HEAD), key_gain.reshape(1, HEAD)]
    specs += [whole(segment_ids.shape), lane_block(part), whole((1, HEAD)), whole((1, HEAD))]
    if part == 1:
        aliases = {len(args) + i: i for i in range(3)}
        args += grads
        specs += [pl.BlockSpec(memory_space=pl.ANY)] * 3
    return pl.pallas_call(
        lambda *refs: attend_kernel(part, *refs),
        grid=(1,),
        in_specs=specs,
        out_specs=[lane_block(part)] * 3 + [whole(part_shape)],
        out_shape=[like, like, like, jax.ShapeDtypeStruct(part_shape, jnp.float32)],
        scratch_shapes=[padded] * 4,
        input_output_aliases=aliases,
        cost_estimate=pl.CostEstimate(
            flops=10**8 * heads, bytes_accessed=5 * 10**5 * heads, transcendentals=10**5 * heads
        ),
    )(*args)


def index(x, z_hi, core):
    return (x * 4 + z_hi) * 2 + core


def turn_by(turn, data):
    pairs = [
        (index(x, z, core), index(x, (z + turn) % TURNS, core))
        for x in range(4)
        for z in range(TURNS)
        for core in range(2)
    ]
    return lax.ppermute(data, "dp", pairs)


def among_peers(data):
    groups = [[index(x, z, core) for x in range(4) for core in range(2)] for z in range(TURNS)]
    return lax.all_to_all(data, "dp", 0, 0, axis_index_groups=groups, tiled=True)


def plane_and_line_groups():
    def flat(x, z_hi, core, y, z_lo):
        return index(x, z_hi, core) * 32 + y * 8 + z_lo

    plane = [
        [flat(x, z_hi, core, y, z_lo) for x in range(4) for y in range(4) for core in range(2)]
        for z_hi in range(4)
        for z_lo in range(8)
    ]
    line = [
        [flat(x, z_hi, core, y, z_lo) for z_hi in range(4) for z_lo in range(8)]
        for x in range(4)
        for y in range(4)
        for core in range(2)
    ]
    return plane, line


def sum_over_all(spread):
    for step, groups in enumerate(plane_and_line_groups()):
        if step:
            spread = jnp.broadcast_to(part, spread.shape)
        spread = lax.all_to_all(
            spread, ("dp", "fsdp"), 0, 0, axis_index_groups=groups, tiled=True
        )
        part = jnp.sum(lax.optimization_barrier(spread), axis=0)
    return part


def on_device(query_in, key_in, value_in, length_plan, segment_ids, out_grad, query_gain, key_gain):
    moved = []
    for part in range(2):
        own, *sends = pack_call(part, length_plan, query_in, key_in, value_in)
        arrived = [own, None, None, None]
        for turn in (1, 3, 2):
            arrived[turn] = turn_by(turn, sends[turn - 1])
        moved.append(arrived)
    shared = (segment_ids, out_grad, query_gain, key_gain)
    got = among_peers(jnp.stack(moved[0], axis=1))
    first = attend_call(0, got, None, *shared)
    last, first = lax.optimization_barrier((moved[1], first))
    got_last = among_peers(jnp.stack(last, axis=1))
    *grads, parts = attend_call(1, got_last, [got, *first], *shared)
    query_total, key_total = sum_over_all(parts)
    return (*grads, query_total, key_total)


def solution(mesh):
    rows = P(("dp", "fsdp"), None)
    return jax.shard_map(
        on_device,
        mesh=mesh,
        in_specs=(rows, rows, rows, rows, rows, rows, P(), P()),
        out_specs=(rows, rows, rows, P(), P()),
        check_vma=False,
    )
```
